256 devices in a mesh: prime: 8 (over z), row: 32 (over x, y, core).
Axes of the slice: x: 4, y: 4, z: 8, core: 2. Of those that a mesh axis runs over, the one named last changes fastest.
Arguments:
- tile_data: bfloat16 [8, 128, 17, 128, 128], P('prime', 'row'), may hold values from -0.125 to 0.125
- tile_slots: int32 [8, 128, 17], P('prime', 'row'), may hold values from 0 to 67, as said below
- requests: int32 [8, 32, 32, 2], P('prime'), may hold values from 0 to 3, as said below
- start_panel: bfloat16 [8, 16384, 128], P('prime', 'row'), may hold values from -6 to 6
- projectors: bfloat16 [8, 16384, 128], P('prime', 'row'), may hold values from -0.09375 to 0.09375
- combine_weights: float32 [8, 8], replicated, may hold values from -2 to 2
Outputs:
- projections_mixed: float32 [8, 6, 128, 128], P(None, None, 'row', 'prime')
- final_panel: bfloat16 [8, 16384, 128], P('prime', 'row')
The draws below stay inside these ranges and needn't reach their ends.
Inputs may be any that keep to these rules, and one draw needn't show every extreme that they name: `tile_slots`: for each system and each device of row, the last slot of each of its 4 block rows is 64 plus the row's index among them, and the other slots of its rows together name each of 0 to 63 exactly once. `requests`: for each system, taking device and source device, the 2 entries are different.
All inputs are finite; a program needn't handle non-finite values.
Results may differ from the reference program's by a relative error of at most 0.02.
Values may be sent and summed in bfloat16 or wider, within the bound.
A program may use at most 64 MiB of HBM per device.

```python
import jax
import jax.numpy as jnp
from jax import lax

TB = 128
W = 128
NB_DEV = 4
C = 2
ITERS = 6
PRIMES = 8
BLOCKS = 128
NQ = 16384
K = 17
N_ROW = 32


def draw_tile_slots(key, part):
    keys = jax.random.split(key, PRIMES * N_ROW)
    orders = jax.vmap(lambda single: jax.random.permutation(single, N_ROW * C))(keys)
    spread = orders.reshape(PRIMES, N_ROW, NB_DEV, N_ROW * C // NB_DEV).astype(jnp.int32)
    diagonal = N_ROW * C + jnp.arange(NB_DEV, dtype=jnp.int32)
    diagonal = jnp.broadcast_to(diagonal[None, None, :, None], (PRIMES, N_ROW, NB_DEV, 1))
    return jnp.concatenate([spread, diagonal], axis=3).reshape(PRIMES, BLOCKS, K).astype(jnp.int32)


def draw_requests(key, part):
    keys = jax.random.split(key, PRIMES * N_ROW * N_ROW)
    orders = jax.vmap(lambda single: jax.random.permutation(single, NB_DEV)[:C])(keys)
    return orders.reshape(PRIMES, N_ROW, N_ROW, C).astype(jnp.int32)


def raised(entries, stream_key, source, target, shards_of, factor):
    def block_of(position):
        return (jnp.arange(entries.shape[position]) // (entries.shape[position] // shards_of)).reshape((-1,) + (1,) * (entries.ndim - 1 - position))

    first = jax.random.permutation(stream_key, shards_of)[block_of(target)]
    other_side = (block_of(target) + shards_of // 2) % shards_of
    return jnp.where((block_of(source) == first) | (block_of(source) == other_side), factor * entries, entries)


def block_scale(rng, extent, shards, low, top_value):
    factor_of, own = 1.0, jax.random.fold_in(rng, 6)
    for axis_at, shards_of in shards:
        heights = jnp.exp(jax.random.uniform(jax.random.fold_in(own, axis_at), (shards_of,), jnp.float32, low / len(shards), top_value / len(shards)))
        factor_of = factor_of * jnp.repeat(heights, extent[axis_at] // shards_of).reshape([-1 if axis == axis_at else 1 for axis in range(len(extent))])
    return factor_of


def gaussian(key, extent, width, most, cuts=(), kind=jnp.bfloat16):
    entries = width * jax.random.normal(key, extent, jnp.float32)
    if cuts:
        entries = entries * block_scale(key, extent, cuts, -0.22, 0.18)
    return jnp.clip(entries, -most, most).astype(kind)


def bell_draw_with(rng, extent, width, bound, shards, heavy, held_as=jnp.bfloat16):
    array = width * jax.random.normal(rng, extent, jnp.float32)
    if shards:
        array = array * block_scale(rng, extent, shards, -0.22, 0.18)
    return jnp.clip(raised(array, jax.random.fold_in(rng, 3), *heavy), -bound, bound).astype(held_as)


def setup_inputs(seed: int = 0) -> dict:
    streams_of = jax.random.split(jax.random.key(seed), 7)
    return {
        "tile_data": gaussian(streams_of[0], (PRIMES, BLOCKS, K, TB, TB), (K * TB) ** -0.5, 0.125, ((0, 8), (1, 32))),
        "tile_slots": draw_tile_slots(jax.random.fold_in(streams_of[6], 71), 0),
        "requests": draw_requests(jax.random.fold_in(streams_of[6], 71), 0),
        "start_panel": gaussian(streams_of[3], (PRIMES, NQ, W), 1.0, 6.0, ((0, 8), (1, 32))),
        "projectors": bell_draw_with(streams_of[4], (PRIMES, NQ, W), NQ ** -0.5, 0.09375, ((0, 8), (1, 32)), (1, 2, 32, 2.75)),
        "combine_weights": gaussian(streams_of[5], (PRIMES, PRIMES), PRIMES ** -0.5, 2.0, (), jnp.float32),
    }


def prime_columns(slot_table, wants):
    owner = (jnp.arange(BLOCKS, dtype=jnp.int32) // NB_DEV)[:, None]
    inside = jnp.clip(slot_table, 0, N_ROW * C - 1).astype(jnp.int32)
    source = inside // C
    within = inside % C
    picked = wants[owner, source, within]
    return jnp.where(slot_table < N_ROW * C, source * NB_DEV + picked, owner * NB_DEV + slot_table - N_ROW * C).astype(jnp.int32)


def one_prime(inputs):
    tiles_here, slots_here, wants_here, start_here, project_here = inputs
    columns = prime_columns(slots_here, wants_here)
    current = start_here
    term_list = []
    for iteration in range(ITERS):
        term_list.append(jnp.dot(project_here.T, current, preferred_element_type=jnp.float32))
        blocks = current.reshape(BLOCKS, TB, W)
        needed = blocks[columns].astype(jnp.float32)
        product = jnp.einsum('ikab,ikbw->iaw', tiles_here.astype(jnp.float32), needed)
        current = product.astype(jnp.bfloat16).reshape(NQ, W)
    return jnp.stack(term_list), current


def reference(tile_data, tile_slots, requests, start_panel, projectors, combine_weights):
    terms, final_panel = lax.map(one_prime, (tile_data, tile_slots, requests, start_panel, projectors))
    mixed = jnp.einsum('qp,pkab->qkab', combine_weights, terms, precision=lax.Precision.HIGHEST)
    return mixed, final_panel
```

```python
import functools

import jax
import jax.numpy as jnp
import numpy as np
from jax import lax
from jax.experimental import pallas as pl
from jax.experimental.pallas import tpu as pltpu
from jax.sharding import PartitionSpec as P

ITERS = 6
TB = 128
MESH = pl.DeviceIdType.MESH

PLACES = (
    (0, 0),
    (3, 0), (1, 0), (0, 3), (0, 1),
    (2, 0), (0, 2), (3, 3), (3, 1), (1, 3), (1, 1),
    (2, 3), (2, 1), (3, 2), (1, 2),
    (2, 2),
)
SLOT = {place: at for at, place in enumerate(PLACES)}
NEAR = 16
ROWS = 512
HALF = 256
EXT = 528


def kernel(meta_ref, weights_ref, tiles_hbm, start_hbm, proj_hbm, mixed_ref, final_ref,
           panel, dense, tiles, proj, spread, columns, acc, terms, others,
           load_sem, prim_send, prim_fwd_send, sec_send, sec_fwd_send, sib_send,
           near_recv, sib_recv, col_send, col_recv, term_send, term_recv):
    z = lax.axis_index("prime")
    r = lax.axis_index("row")
    c = lax.rem(r, 2)
    y = lax.rem(r // 2, 4)
    x = r // 8

    def row_at(da, db):
        x_at = lax.rem(x + da * (1 - c) + db * c, 4)
        y_at = lax.rem(y + da * c + db * (1 - c), 4)
        return (x_at * 4 + y_at) * 2 + c

    a_up, a_down = (z, row_at(1, 0)), (z, row_at(3, 0))
    b_up, b_down = (z, row_at(0, 1)), (z, row_at(0, 3))
    sibling = (z, r + 1 - 2 * c)

    barrier = pltpu.get_barrier_semaphore()

    @pl.loop(1, 32)
    def _(d):
        pl.semaphore_signal(barrier, inc=1, device_id=(z, lax.rem(r + d, 32)), device_id_type=MESH)

    @pl.loop(1, 8)
    def _(d):
        pl.semaphore_signal(barrier, inc=1, device_id=(lax.rem(z + d, 8), r), device_id_type=MESH)

    load_proj = pltpu.make_async_copy(proj_hbm, proj, load_sem.at[0])
    load_start = pltpu.make_async_copy(start_hbm, panel.at[0, 0], load_sem.at[1])
    load_tiles = pltpu.make_async_copy(tiles_hbm, tiles, load_sem.at[2])
    load_proj.start()
    load_start.start()
    load_tiles.start()

    load_proj.wait()
    at_row = lax.broadcasted_iota(jnp.int32, (ROWS, ROWS), 0)
    at_col = lax.broadcasted_iota(jnp.int32, (ROWS, ROWS), 1)
    wanted = ((at_row >> 2) & 3) * TB + (at_row >> 4) * 4 + (at_row & 3)
    choose = jnp.where(at_col == wanted, 1.0, 0.0).astype(jnp.bfloat16)
    wide = jnp.concatenate([proj[pl.ds(q * TB, TB), :] for q in range(4)], axis=1)
    spread[...] = lax.dot_general(
        choose, wide, (((1,), (1,)), ((), ())), preferred_element_type=jnp.float32
    ).astype(jnp.bfloat16)

    pl.semaphore_wait(barrier, 38)

    def column_copy(d):
        to = lax.rem(r + d, 32)
        return pltpu.make_async_remote_copy(
            src_ref=spread.at[pl.ds(pl.multiple_of(to * 16, 16), 16)],
            dst_ref=columns.at[d],
            send_sem=col_send.at[d], recv_sem=col_recv.at[d],
            device_id=(z, to), device_id_type=MESH)

    @pl.loop(1, 32)
    def _(d):
        column_copy(d).start()

    columns[0] = spread[pl.ds(pl.multiple_of(r * 16, 16), 16), :]
    load_start.wait()
    load_tiles.wait()

    def build(slot):
        key = [meta_ref[64 + 2 * slot + which] for which in range(2)]
        tile = [tiles[meta_ref[2 * slot + which]] for which in range(2)]
        for i in range(4):
            for b in range(4):
                here = jnp.where(key[0] == i * 4 + b, tile[0],
                                 jnp.where(key[1] == i * 4 + b, tile[1], jnp.zeros_like(tile[1])))
                dense[slot, pl.ds(i * TB, TB), pl.ds(b * TB, TB)] = here
        part = columns[meta_ref[128 + slot]].astype(jnp.float32)
        band = lax.broadcasted_iota(jnp.int32, (16, TB), 0) >> 2
        for q in range(4):
            dense[slot, pl.ds(ROWS, 16), pl.ds(q * TB, TB)] = jnp.where(
                band == q, part, 0.0).astype(jnp.bfloat16)

    @pl.loop(0, ITERS)
    def _(t):
        par = lax.rem(t, 2)

        def piece(slot, h):
            return panel.at[par, slot, pl.ds(h * HALF, HALF)]

        def near(src, dst, h, send_sem, to):
            return pltpu.make_async_remote_copy(
                src_ref=piece(SLOT[src], h), dst_ref=piece(SLOT[dst], h),
                send_sem=send_sem, recv_sem=near_recv.at[par, SLOT[dst], h],
                device_id=to, device_id_type=MESH)

        prim = {}
        for h in range(2):
            prim[(3, 0), h] = near((0, 0), (3, 0), h, prim_send.at[0, h], a_up)
            prim[(1, 0), h] = near((0, 0), (1, 0), h, prim_send.at[1, h], a_down)
        prim[(2, 0), 0] = near((3, 0), (2, 0), 0, prim_fwd_send.at[0], a_up)
        prim[(2, 0), 1] = near((1, 0), (2, 0), 1, prim_fwd_send.at[1], a_down)
        sec = {}
        for k in range(4):
            for h in range(2):
                sec[(k, 3), h] = near((k, 0), (k, 3), h, sec_send.at[k, 0, h], b_up)
                sec[(k, 1), h] = near((k, 0), (k, 1), h, sec_send.at[k, 1, h], b_down)
            sec[(k, 2), 0] = near((k, 3), (k, 2), 0, sec_fwd_send.at[k, 0], b_up)
            sec[(k, 2), 1] = near((k, 1), (k, 2), 1, sec_fwd_send.at[k, 1], b_down)
        got = {**prim, **sec}
        sib = {}
        for place in PLACES:
            for h in range(2):
                sib[place, h] = pltpu.make_async_remote_copy(
                    src_ref=piece(SLOT[place], h), dst_ref=piece(NEAR + SLOT[place], h),
                    send_sem=sib_send.at[SLOT[place], h],
                    recv_sem=sib_recv.at[par, SLOT[place], h],
                    device_id=sibling, device_id_type=MESH)

        def pass_on(place, h):
            got[place, h].wait_recv()
            da, db = place
            if place == (3, 0) and h == 0:
                got[(2, 0), 0].start()
            if place == (1, 0) and h == 1:
                got[(2, 0), 1].start()
            if db == 0:
                first, second = ((da, 3), (da, 1)) if h == 0 else ((da, 1), (da, 3))
                got[first, h].start()
                got[second, h].start()
            if db == 3 and h == 0:
                got[(da, 2), 0].start()
            if db == 1 and h == 1:
                got[(da, 2), 1].start()
            sib[place, h].start()

        def add_up(low, high):
            def body(slot, carry):
                @pl.when(t == 0)
                def _():
                    build(slot)
                acc[...] += jnp.dot(dense[slot], panel[par, slot], preferred_element_type=jnp.float32)
                return carry
            lax.fori_loop(low, high, body, None)

        def take_sibling(places):
            for place in places:
                for h in range(2):
                    sib[place, h].wait_recv()

        prim[(3, 0), 0].start()
        prim[(1, 0), 1].start()
        prim[(3, 0), 1].start()
        prim[(1, 0), 0].start()
        sec[(0, 3), 0].start()
        sec[(0, 1), 1].start()
        sec[(0, 3), 1].start()
        sec[(0, 1), 0].start()
        for h in range(2):
            sib[(0, 0), h].start()

        for i in range(4):
            acc[pl.ds(i * TB, TB), :] = jnp.dot(
                tiles[i * 17 + 16], panel[par, 0, pl.ds(i * TB, TB), :],
                preferred_element_type=jnp.float32)
        acc[pl.ds(ROWS, 16), :] = jnp.zeros((16, TB), jnp.float32)

        @pl.when(t == 0)
        def _():
            @pl.loop(1, 32)
            def _(d):
                column_copy(d).wait()

        add_up(0, 1)
        one, two, three, four = PLACES[1:5], PLACES[5:11], PLACES[11:15], PLACES[15:]
        pass_on((3, 0), 0)
        pass_on((1, 0), 1)
        pass_on((3, 0), 1)
        pass_on((1, 0), 0)
        pass_on((0, 3), 0)
        pass_on((0, 1), 1)
        pass_on((0, 3), 1)
        pass_on((0, 1), 0)
        take_sibling(PLACES[:1])
        add_up(NEAR, NEAR + 1)
        pass_on((2, 0), 0)
        pass_on((2, 0), 1)
        add_up(1, 5)
        for place in two[1:]:
            for h in (0, 1):
                pass_on(place, h)
        take_sibling(one)
        add_up(NEAR + 1, NEAR + 5)
        add_up(5, 11)
        for place in three:
            for h in (0, 1):
                pass_on(place, h)
        take_sibling(two)
        add_up(NEAR + 5, NEAR + 11)
        add_up(11, 15)
        for h in (0, 1):
            pass_on((2, 2), h)
        take_sibling(three)
        add_up(NEAR + 11, NEAR + 15)
        add_up(15, 16)
        take_sibling(four)
        add_up(NEAR + 15, NEAR + 16)

        for copy in list(got.values()) + list(sib.values()):
            copy.wait_send()

        panel[1 - par, 0] = acc[pl.ds(0, ROWS), :].astype(jnp.bfloat16)
        low = acc[pl.ds(ROWS, 8), :] + acc[pl.ds(ROWS + 8, 8), :]
        terms[t] = low + pltpu.roll(low, 4, 0)

    def term_copy(d):
        return pltpu.make_async_remote_copy(
            src_ref=terms, dst_ref=others.at[d],
            send_sem=term_send.at[d], recv_sem=term_recv.at[d],
            device_id=(lax.rem(z + d, 8), r), device_id_type=MESH)

    for d in range(1, 8):
        term_copy(d).start()
    final_ref[...] = panel[ITERS % 2, 0]
    others[0] = terms[...]
    for d in range(1, 8):
        term_copy(d).wait()
    for q in range(8):
        total = jnp.zeros((ITERS, 8, TB), jnp.float32)
        for d in range(8):
            total += weights_ref[q, lax.rem(z + 8 - d, 8)] * others[d]
        mixed_ref[q] = total


def shards(tile_data, tile_slots, requests, start_panel, projectors, combine_weights):
    z = lax.axis_index("prime")
    r = lax.axis_index("row")
    c = r % 2
    y = (r // 2) % 4
    x = r // 8
    da = jnp.asarray(np.array([place[0] for place in PLACES] * 2, np.int32))
    db = jnp.asarray(np.array([place[1] for place in PLACES] * 2, np.int32))
    core = jnp.where(jnp.arange(32) < NEAR, c, 1 - c)
    x_at = (x + da * (1 - core) + db * core) % 4
    y_at = (y + da * core + db * (1 - core)) % 4
    source = (x_at * 4 + y_at) * 2 + core
    names = (source[:, None] * 2 + jnp.arange(2)[None, :]).reshape(64)
    flat_slots = tile_slots.reshape(68)
    spots = jnp.arange(68, dtype=jnp.int32)
    where_is = jnp.sum(jnp.where(flat_slots[None, :] == names[:, None], spots[None, :], 0), axis=1)
    own_wants = lax.dynamic_index_in_dim(requests, r, 1, keepdims=False).reshape(64)
    pick = jnp.sum(jnp.where(jnp.arange(64)[None, :] == names[:, None], own_wants[None, :], 0), axis=1)
    meta = jnp.concatenate([where_is, where_is // 17 * 4 + pick, (r - source + 32) % 32]).astype(jnp.int32)
    anywhere = pl.BlockSpec(memory_space=pl.ANY)
    small = pl.BlockSpec(memory_space=pltpu.SMEM)
    full = pl.BlockSpec(memory_space=pltpu.VMEM)
    dma = pltpu.SemaphoreType.DMA
    mixed, final = pl.pallas_call(
        kernel,
        out_shape=(
            jax.ShapeDtypeStruct((8, ITERS, 8, TB), jnp.float32),
            jax.ShapeDtypeStruct((ROWS, TB), jnp.bfloat16),
        ),
        in_specs=[small, small, anywhere, anywhere, anywhere],
        out_specs=(full, full),
        scratch_shapes=[
            pltpu.VMEM((2, 32, ROWS, TB), jnp.bfloat16),
            pltpu.VMEM((32, EXT, ROWS), jnp.bfloat16),
            pltpu.VMEM((68, TB, TB), jnp.bfloat16),
            pltpu.VMEM((ROWS, TB), jnp.bfloat16),
            pltpu.VMEM((ROWS, TB), jnp.bfloat16),
            pltpu.VMEM((32, 16, TB), jnp.bfloat16),
            pltpu.VMEM((EXT, TB), jnp.float32),
            pltpu.VMEM((ITERS, 8, TB), jnp.float32),
            pltpu.VMEM((8, ITERS, 8, TB), jnp.float32),
            dma((3,)), dma((2, 2)), dma((2,)), dma((4, 2, 2)), dma((4, 2)), dma((16, 2)),
            dma((2, 16, 2)), dma((2, 16, 2)), dma((32,)), dma((32,)), dma((8,)), dma((8,)),
        ],
        compiler_params=pltpu.CompilerParams(collective_id=0, has_side_effects=True),
    )(meta, combine_weights, tile_data.reshape(68, TB, TB), start_panel.reshape(ROWS, TB),
      projectors.reshape(ROWS, TB))
    mine = lax.dynamic_slice(mixed, (0, 0, 0, z * 16), (8, ITERS, 4, 16))
    return mine, final.reshape(1, ROWS, TB)


def solution(mesh):
    return jax.shard_map(
        shards,
        mesh=mesh,
        in_specs=(
            P("prime", "row", None, None, None),
            P("prime", "row", None),
            P("prime", None, None, None),
            P("prime", "row", None),
            P("prime", "row", None),
            P(),
        ),
        out_specs=(P(None, None, "row", "prime"), P("prime", "row", None)),
        check_vma=False,
    )
```

```python
import functools

import jax
import jax.numpy as jnp
import numpy as np
from jax import lax
from jax.experimental import pallas as pl
from jax.experimental.pallas import tpu as pltpu
from jax.sharding import PartitionSpec as P

ITERS = 6
TB = 128
MESH = pl.DeviceIdType.MESH

PLACES = (
    (0, 0),
    (3, 0), (1, 0), (0, 3), (0, 1),
    (2, 0), (0, 2), (3, 3), (3, 1), (1, 3), (1, 1),
    (2, 3), (2, 1), (3, 2), (1, 2),
    (2, 2),
)
SLOT = {place: at for at, place in enumerate(PLACES)}
NEAR = 16
ROWS = 512
HALF = 256
EXT = 528


def kernel(meta_ref, weights_ref, tiles_hbm, start_hbm, proj_hbm, mixed_ref, final_ref,
           panel, bands, tiles, proj, spread, columns, acc, terms, others,
           load_sem, prim_send, prim_fwd_send, sec_send, sec_fwd_send, sib_send,
           near_recv, sib_recv, col_send, col_recv, term_send, term_recv):
    z = lax.axis_index("prime")
    r = lax.axis_index("row")
    c = lax.rem(r, 2)
    y = lax.rem(r // 2, 4)
    x = r // 8

    def row_at(da, db):
        x_at = lax.rem(x + da * (1 - c) + db * c, 4)
        y_at = lax.rem(y + da * c + db * (1 - c), 4)
        return (x_at * 4 + y_at) * 2 + c

    a_up, a_down = (z, row_at(1, 0)), (z, row_at(3, 0))
    b_up, b_down = (z, row_at(0, 1)), (z, row_at(0, 3))
    sibling = (z, r + 1 - 2 * c)

    barrier = pltpu.get_barrier_semaphore()

    @pl.loop(1, 32)
    def _(d):
        pl.semaphore_signal(barrier, inc=1, device_id=(z, lax.rem(r + d, 32)), device_id_type=MESH)

    @pl.loop(1, 8)
    def _(d):
        pl.semaphore_signal(barrier, inc=1, device_id=(lax.rem(z + d, 8), r), device_id_type=MESH)

    load_proj = pltpu.make_async_copy(proj_hbm, proj, load_sem.at[0])
    load_start = pltpu.make_async_copy(start_hbm, panel.at[0, 0], load_sem.at[1])
    load_tiles = pltpu.make_async_copy(tiles_hbm, tiles, load_sem.at[2])
    load_proj.start()
    load_start.start()
    load_tiles.start()

    load_proj.wait()
    at_row = lax.broadcasted_iota(jnp.int32, (ROWS, ROWS), 0)
    at_col = lax.broadcasted_iota(jnp.int32, (ROWS, ROWS), 1)
    wanted = ((at_row >> 2) & 3) * TB + (at_row >> 4) * 4 + (at_row & 3)
    choose = jnp.where(at_col == wanted, 1.0, 0.0).astype(jnp.bfloat16)
    wide = jnp.concatenate([proj[pl.ds(q * TB, TB), :] for q in range(4)], axis=1)
    spread[...] = lax.dot_general(
        choose, wide, (((1,), (1,)), ((), ())), preferred_element_type=jnp.float32
    ).astype(jnp.bfloat16)

    pl.semaphore_wait(barrier, 38)

    def column_copy(d):
        to = lax.rem(r + d, 32)
        return pltpu.make_async_remote_copy(
            src_ref=spread.at[pl.ds(pl.multiple_of(to * 16, 16), 16)],
            dst_ref=columns.at[d],
            send_sem=col_send.at[d], recv_sem=col_recv.at[d],
            device_id=(z, to), device_id_type=MESH)

    columns[0] = spread[pl.ds(pl.multiple_of(r * 16, 16), 16), :]
    load_start.wait()
    load_tiles.wait()

    def build(slot):
        part = columns[meta_ref[128 + slot]].astype(jnp.float32)
        band = lax.broadcasted_iota(jnp.int32, (16, TB), 0) >> 2
        for q in range(4):
            bands[slot, :, pl.ds(q * TB, TB)] = jnp.where(
                band == q, part, 0.0).astype(jnp.bfloat16)

    def term_copy(d, t):
        return pltpu.make_async_remote_copy(
            src_ref=terms.at[t], dst_ref=others.at[d, t],
            send_sem=term_send.at[d, t], recv_sem=term_recv.at[d, t],
            device_id=(lax.rem(z + d, 8), r), device_id_type=MESH)

    def copies(par):
        def piece(slot, h):
            return panel.at[par, slot, pl.ds(h * HALF, HALF)]

        def near(src, dst, h, send_sem, to):
            return pltpu.make_async_remote_copy(
                src_ref=piece(SLOT[src], h), dst_ref=piece(SLOT[dst], h),
                send_sem=send_sem, recv_sem=near_recv.at[par, SLOT[dst], h],
                device_id=to, device_id_type=MESH)

        got = {}
        for h in range(2):
            got[(3, 0), h] = near((0, 0), (3, 0), h, prim_send.at[par, 0, h], a_up)
            got[(1, 0), h] = near((0, 0), (1, 0), h, prim_send.at[par, 1, h], a_down)
        got[(2, 0), 0] = near((3, 0), (2, 0), 0, prim_fwd_send.at[par, 0], a_up)
        got[(2, 0), 1] = near((1, 0), (2, 0), 1, prim_fwd_send.at[par, 1], a_down)
        for k in range(4):
            for h in range(2):
                got[(k, 3), h] = near((k, 0), (k, 3), h, sec_send.at[par, k, 0, h], b_up)
                got[(k, 1), h] = near((k, 0), (k, 1), h, sec_send.at[par, k, 1, h], b_down)
            got[(k, 2), 0] = near((k, 3), (k, 2), 0, sec_fwd_send.at[par, k, 0], b_up)
            got[(k, 2), 1] = near((k, 1), (k, 2), 1, sec_fwd_send.at[par, k, 1], b_down)
        sib = {}
        for place in PLACES:
            for h in range(2):
                sib[place, h] = pltpu.make_async_remote_copy(
                    src_ref=piece(SLOT[place], h), dst_ref=piece(NEAR + SLOT[place], h),
                    send_sem=sib_send.at[par, SLOT[place], h],
                    recv_sem=sib_recv.at[par, SLOT[place], h],
                    device_id=sibling, device_id_type=MESH)
        return got, sib

    def finish_sends(par):
        got, sib = copies(par)
        for copy in list(got.values()) + list(sib.values()):
            copy.wait_send()

    @pl.loop(0, ITERS)
    def _(t):
        par = lax.rem(t, 2)

        got, sib = copies(par)

        def pass_on(place, h):
            got[place, h].wait_recv()
            da, db = place
            if place == (3, 0) and h == 0:
                got[(2, 0), 0].start()
            if place == (1, 0) and h == 1:
                got[(2, 0), 1].start()
            if db == 0:
                first, second = ((da, 3), (da, 1)) if h == 0 else ((da, 1), (da, 3))
                got[first, h].start()
                got[second, h].start()
            if db == 3 and h == 0:
                got[(da, 2), 0].start()
            if db == 1 and h == 1:
                got[(da, 2), 1].start()
            sib[place, h].start()

        def products(slot):
            parts = [panel[par, slot, pl.ds(b * TB, TB), :] for b in range(4)]
            found = []
            for which in range(2):
                key = meta_ref[64 + 2 * slot + which]
                pick = key & 3
                block = jnp.where(pick == 0, parts[0], jnp.where(
                    pick == 1, parts[1], jnp.where(pick == 2, parts[2], parts[3])))
                found.append((key >> 2, jnp.dot(
                    tiles[meta_ref[2 * slot + which]], block, preferred_element_type=jnp.float32)))
            term = jnp.dot(bands[slot], panel[par, slot], preferred_element_type=jnp.float32)
            return found, term

        def add_up(low, high):
            step = 2 - (high - low) % 2

            def body(at, carry):
                slots = [low + at * step + n for n in range(step)]

                @pl.when(t == 0)
                def _():
                    for slot in slots:
                        build(slot)
                found, term = [], None
                for slot in slots:
                    more, part = products(slot)
                    found += more
                    term = part if term is None else term + part
                acc[pl.ds(ROWS, 16), :] += term
                for i in range(4):
                    total = acc[pl.ds(i * TB, TB), :]
                    for row, product in found:
                        total = total + jnp.where(row == i, product, 0.0)
                    acc[pl.ds(i * TB, TB), :] = total
                return carry
            lax.fori_loop(0, (high - low) // step, body, None)

        def take_sibling(places):
            for place in places:
                for h in range(2):
                    sib[place, h].wait_recv()

        got[(3, 0), 0].start()
        got[(1, 0), 1].start()
        got[(3, 0), 1].start()
        got[(1, 0), 0].start()
        got[(0, 3), 0].start()
        got[(0, 1), 1].start()
        got[(0, 3), 1].start()
        got[(0, 1), 0].start()
        for h in range(2):
            sib[(0, 0), h].start()

        @pl.when(t == 0)
        def _():
            @pl.loop(1, 32)
            def _(d):
                column_copy(d).start()

        @pl.when(t > 0)
        def _():
            for d in range(1, 8):
                term_copy(d, t - 1).start()

        for i in range(4):
            acc[pl.ds(i * TB, TB), :] = jnp.dot(
                tiles[i * 17 + 16], panel[par, 0, pl.ds(i * TB, TB), :],
                preferred_element_type=jnp.float32)
        acc[pl.ds(ROWS, 16), :] = jnp.zeros((16, TB), jnp.float32)

        @pl.when(t == 0)
        def _():
            @pl.loop(1, 32)
            def _(d):
                column_copy(d).wait()

        add_up(0, 1)

        @pl.when(t > 0)
        def _():
            finish_sends(1 - par)

        one, two, three, four = PLACES[1:5], PLACES[5:11], PLACES[11:15], PLACES[15:]
        pass_on((3, 0), 0)
        pass_on((1, 0), 1)
        pass_on((3, 0), 1)
        pass_on((1, 0), 0)
        pass_on((0, 3), 0)
        pass_on((0, 1), 1)
        pass_on((0, 3), 1)
        pass_on((0, 1), 0)
        take_sibling(PLACES[:1])
        add_up(NEAR, NEAR + 1)
        pass_on((2, 0), 0)
        pass_on((2, 0), 1)
        add_up(1, 5)
        for place in two[1:]:
            for h in (0, 1):
                pass_on(place, h)
        take_sibling(one)
        add_up(NEAR + 1, NEAR + 5)
        add_up(5, 11)
        for place in three:
            for h in (0, 1):
                pass_on(place, h)
        take_sibling(two)
        add_up(NEAR + 5, NEAR + 11)
        add_up(11, 15)
        for h in (0, 1):
            pass_on((2, 2), h)
        take_sibling(three)
        add_up(NEAR + 11, NEAR + 15)
        add_up(15, 16)
        take_sibling(four)
        add_up(NEAR + 15, NEAR + 16)

        panel[1 - par, 0] = acc[pl.ds(0, ROWS), :].astype(jnp.bfloat16)
        low = acc[pl.ds(ROWS, 8), :] + acc[pl.ds(ROWS + 8, 8), :]
        terms[t] = low + pltpu.roll(low, 4, 0)

    for d in range(1, 8):
        term_copy(d, ITERS - 1).start()
    final_ref[...] = panel[ITERS % 2, 0]
    others[0] = terms[...]
    finish_sends((ITERS - 1) % 2)

    @pl.loop(0, ITERS)
    def _(t):
        for d in range(1, 8):
            term_copy(d, t).wait()
    turn = lax.rem(TB - z * 16, TB)
    for q in range(8):
        total = jnp.zeros((ITERS, 8, TB), jnp.float32)
        for d in range(8):
            total += weights_ref[q, lax.rem(z + 8 - d, 8)] * others[d]
        mixed_ref[q] = pltpu.roll(total, turn, 2)[:, :4, :16]


def shards(tile_data, tile_slots, requests, start_panel, projectors, combine_weights):
    r = lax.axis_index("row")
    c = r % 2
    y = (r // 2) % 4
    x = r // 8
    da = jnp.asarray(np.array([place[0] for place in PLACES] * 2, np.int32))
    db = jnp.asarray(np.array([place[1] for place in PLACES] * 2, np.int32))
    core = jnp.where(jnp.arange(32) < NEAR, c, 1 - c)
    x_at = (x + da * (1 - core) + db * core) % 4
    y_at = (y + da * core + db * (1 - core)) % 4
    source = (x_at * 4 + y_at) * 2 + core
    names = (source[:, None] * 2 + jnp.arange(2)[None, :]).reshape(64)
    flat_slots = tile_slots.reshape(68)
    spots = jnp.arange(68, dtype=jnp.int32)
    where_is = jnp.sum(jnp.where(flat_slots[None, :] == names[:, None], spots[None, :], 0), axis=1)
    own_wants = lax.dynamic_index_in_dim(requests, r, 1, keepdims=False).reshape(64)
    pick = jnp.sum(jnp.where(jnp.arange(64)[None, :] == names[:, None], own_wants[None, :], 0), axis=1)
    meta = jnp.concatenate([where_is, where_is // 17 * 4 + pick, (r - source + 32) % 32]).astype(jnp.int32)
    anywhere = pl.BlockSpec(memory_space=pl.ANY)
    small = pl.BlockSpec(memory_space=pltpu.SMEM)
    full = pl.BlockSpec(memory_space=pltpu.VMEM)
    dma = pltpu.SemaphoreType.DMA
    mixed, final = pl.pallas_call(
        kernel,
        out_shape=(
            jax.ShapeDtypeStruct((8, ITERS, 4, 16), jnp.float32),
            jax.ShapeDtypeStruct((ROWS, TB), jnp.bfloat16),
        ),
        in_specs=[small, small, anywhere, anywhere, anywhere],
        out_specs=(full, full),
        scratch_shapes=[
            pltpu.VMEM((2, 32, ROWS, TB), jnp.bfloat16),
            pltpu.VMEM((32, 16, ROWS), jnp.bfloat16),
            pltpu.VMEM((68, TB, TB), jnp.bfloat16),
            pltpu.VMEM((ROWS, TB), jnp.bfloat16),
            pltpu.VMEM((ROWS, TB), jnp.bfloat16),
            pltpu.VMEM((32, 16, TB), jnp.bfloat16),
            pltpu.VMEM((EXT, TB), jnp.float32),
            pltpu.VMEM((ITERS, 8, TB), jnp.float32),
            pltpu.VMEM((8, ITERS, 8, TB), jnp.float32),
            dma((3,)), dma((2, 2, 2)), dma((2, 2)), dma((2, 4, 2, 2)), dma((2, 4, 2)), dma((2, 16, 2)),
            dma((2, 16, 2)), dma((2, 16, 2)), dma((32,)), dma((32,)), dma((8, ITERS)), dma((8, ITERS)),
        ],
        compiler_params=pltpu.CompilerParams(collective_id=0, has_side_effects=True),
    )(meta, combine_weights, tile_data.reshape(68, TB, TB), start_panel.reshape(ROWS, TB),
      projectors.reshape(ROWS, TB))
    return mixed, final.reshape(1, ROWS, TB)


def solution(mesh):
    return jax.shard_map(
        shards,
        mesh=mesh,
        in_specs=(
            P("prime", "row", None, None, None),
            P("prime", "row", None),
            P("prime", None, None, None),
            P("prime", "row", None),
            P("prime", "row", None),
            P(),
        ),
        out_specs=(P(None, None, "row", "prime"), P("prime", "row", None)),
        check_vma=False,
    )
```

```python
import functools

import jax
import jax.numpy as jnp
import numpy as np
from jax import lax
from jax.experimental import pallas as pl
from jax.experimental.pallas import tpu as pltpu
from jax.sharding import PartitionSpec as P

ITERS = 6
TB = 128
MESH = pl.DeviceIdType.MESH

PLACES = (
    (0, 0),
    (3, 0), (1, 0), (0, 3), (0, 1),
    (2, 0), (0, 2), (3, 3), (3, 1), (1, 3), (1, 1),
    (2, 3), (2, 1), (3, 2), (1, 2),
    (2, 2),
)
SLOT = {place: at for at, place in enumerate(PLACES)}
NEAR = 16
ROWS = 512
HALF = 256
EXT = 528


def kernel(meta_ref, weights_ref, tiles_hbm, start_hbm, proj_hbm, mixed_ref, final_ref,
           panel, bands, tiles, proj, spread, columns, acc, terms, others,
           load_sem, prim_send, prim_fwd_send, sec_send, sec_fwd_send, sib_send,
           near_recv, sib_recv, col_send, col_recv, term_send, term_recv):
    z = lax.axis_index("prime")
    r = lax.axis_index("row")
    c = lax.rem(r, 2)
    y = lax.rem(r // 2, 4)
    x = r // 8

    def row_at(da, db):
        x_at = lax.rem(x + da * (1 - c) + db * c, 4)
        y_at = lax.rem(y + da * c + db * (1 - c), 4)
        return (x_at * 4 + y_at) * 2 + c

    a_up, a_down = (z, row_at(1, 0)), (z, row_at(3, 0))
    b_up, b_down = (z, row_at(0, 1)), (z, row_at(0, 3))
    sibling = (z, r + 1 - 2 * c)

    barrier = pltpu.get_barrier_semaphore()

    @pl.loop(1, 32)
    def _(d):
        pl.semaphore_signal(barrier, inc=1, device_id=(z, lax.rem(r + d, 32)), device_id_type=MESH)

    @pl.loop(1, 8)
    def _(d):
        pl.semaphore_signal(barrier, inc=1, device_id=(lax.rem(z + d, 8), r), device_id_type=MESH)

    load_proj = pltpu.make_async_copy(proj_hbm, proj, load_sem.at[0])
    load_start = pltpu.make_async_copy(start_hbm, panel.at[0, 0], load_sem.at[1])
    load_tiles = pltpu.make_async_copy(tiles_hbm, tiles, load_sem.at[2])
    load_proj.start()
    load_start.start()
    load_tiles.start()

    load_proj.wait()
    at_row = lax.broadcasted_iota(jnp.int32, (ROWS, ROWS), 0)
    at_col = lax.broadcasted_iota(jnp.int32, (ROWS, ROWS), 1)
    wanted = ((at_row >> 2) & 3) * TB + (at_row >> 4) * 4 + (at_row & 3)
    choose = jnp.where(at_col == wanted, 1.0, 0.0).astype(jnp.bfloat16)
    wide = jnp.concatenate([proj[pl.ds(q * TB, TB), :] for q in range(4)], axis=1)
    spread[...] = lax.dot_general(
        choose, wide, (((1,), (1,)), ((), ())), preferred_element_type=jnp.float32
    ).astype(jnp.bfloat16)

    pl.semaphore_wait(barrier, 38)

    def column_copy(d):
        to = lax.rem(r + d, 32)
        return pltpu.make_async_remote_copy(
            src_ref=spread.at[pl.ds(pl.multiple_of(to * 16, 16), 16)],
            dst_ref=columns.at[d],
            send_sem=col_send.at[d], recv_sem=col_recv.at[d],
            device_id=(z, to), device_id_type=MESH)

    columns[0] = spread[pl.ds(pl.multiple_of(r * 16, 16), 16), :]
    load_start.wait()
    load_tiles.wait()

    def build(slot):
        part = columns[meta_ref[128 + slot]].astype(jnp.float32)
        band = lax.broadcasted_iota(jnp.int32, (16, TB), 0) >> 2
        for q in range(4):
            bands[slot, :, pl.ds(q * TB, TB)] = jnp.where(
                band == q, part, 0.0).astype(jnp.bfloat16)

    def term_copy(d, t):
        return pltpu.make_async_remote_copy(
            src_ref=terms.at[t], dst_ref=others.at[d, t],
            send_sem=term_send.at[d, t], recv_sem=term_recv.at[d, t],
            device_id=(lax.rem(z + d, 8), r), device_id_type=MESH)

    def copies(par):
        def piece(slot, h):
            return panel.at[par, slot, pl.ds(h * HALF, HALF)]

        def near(src, dst, h, send_sem, to):
            return pltpu.make_async_remote_copy(
                src_ref=piece(SLOT[src], h), dst_ref=piece(SLOT[dst], h),
                send_sem=send_sem, recv_sem=near_recv.at[par, SLOT[dst], h],
                device_id=to, device_id_type=MESH)

        got = {}
        for h in range(2):
            got[(3, 0), h] = near((0, 0), (3, 0), h, prim_send.at[par, 0, h], a_up)
            got[(1, 0), h] = near((0, 0), (1, 0), h, prim_send.at[par, 1, h], a_down)
        got[(2, 0), 0] = near((3, 0), (2, 0), 0, prim_fwd_send.at[par, 0], a_up)
        got[(2, 0), 1] = near((1, 0), (2, 0), 1, prim_fwd_send.at[par, 1], a_down)
        for k in range(4):
            for h in range(2):
                got[(k, 3), h] = near((k, 0), (k, 3), h, sec_send.at[par, k, 0, h], b_up)
                got[(k, 1), h] = near((k, 0), (k, 1), h, sec_send.at[par, k, 1, h], b_down)
            got[(k, 2), 0] = near((k, 3), (k, 2), 0, sec_fwd_send.at[par, k, 0], b_up)
            got[(k, 2), 1] = near((k, 1), (k, 2), 1, sec_fwd_send.at[par, k, 1], b_down)
        sib = {}
        for place in PLACES:
            for h in range(2):
                sib[place, h] = pltpu.make_async_remote_copy(
                    src_ref=piece(SLOT[place], h), dst_ref=piece(NEAR + SLOT[place], h),
                    send_sem=sib_send.at[par, SLOT[place], h],
                    recv_sem=sib_recv.at[par, SLOT[place], h],
                    device_id=sibling, device_id_type=MESH)
        return got, sib

    def finish_sends(par):
        got, sib = copies(par)
        for copy in list(got.values()) + list(sib.values()):
            copy.wait_send()

    @pl.loop(0, ITERS)
    def _(t):
        par = lax.rem(t, 2)

        got, sib = copies(par)

        def pass_on(place, h):
            got[place, h].wait_recv()
            da, db = place
            if place == (3, 0) and h == 0:
                got[(2, 0), 0].start()
            if place == (1, 0) and h == 1:
                got[(2, 0), 1].start()
            if db == 0:
                first, second = ((da, 3), (da, 1)) if h == 0 else ((da, 1), (da, 3))
                got[first, h].start()
                got[second, h].start()
            if db == 3 and h == 0:
                got[(da, 2), 0].start()
            if db == 1 and h == 1:
                got[(da, 2), 1].start()
            sib[place, h].start()

        def products(slot):
            parts = [panel[par, slot, pl.ds(b * TB, TB), :] for b in range(4)]
            found = []
            for which in range(2):
                key = meta_ref[64 + 2 * slot + which]
                pick = key & 3
                block = jnp.where(pick == 0, parts[0], jnp.where(
                    pick == 1, parts[1], jnp.where(pick == 2, parts[2], parts[3])))
                found.append((key >> 2, jnp.dot(
                    tiles[meta_ref[2 * slot + which]], block, preferred_element_type=jnp.float32)))
            term = jnp.dot(bands[slot], panel[par, slot], preferred_element_type=jnp.float32)
            return found, term

        def add_up(low, high):
            step = 2 - (high - low) % 2

            def body(at, carry):
                slots = [low + at * step + n for n in range(step)]

                @pl.when(t == 0)
                def _():
                    for slot in slots:
                        build(slot)
                found, term = [], None
                for slot in slots:
                    more, part = products(slot)
                    found += more
                    term = part if term is None else term + part
                acc[pl.ds(ROWS, 16), :] += term
                for i in range(4):
                    total = acc[pl.ds(i * TB, TB), :]
                    for row, product in found:
                        total = total + jnp.where(row == i, product, 0.0)
                    acc[pl.ds(i * TB, TB), :] = total
                return carry
            lax.fori_loop(0, (high - low) // step, body, None)

        def take_sibling(places):
            for place in places:
                for h in range(2):
                    sib[place, h].wait_recv()

        got[(3, 0), 0].start()
        got[(1, 0), 1].start()
        got[(3, 0), 1].start()
        got[(1, 0), 0].start()
        got[(0, 3), 0].start()
        got[(0, 1), 1].start()
        got[(0, 3), 1].start()
        got[(0, 1), 0].start()
        for h in range(2):
            sib[(0, 0), h].start()

        @pl.when(t == 0)
        def _():
            @pl.loop(1, 32)
            def _(d):
                column_copy(d).start()

        @pl.when(t > 0)
        def _():
            for d in range(1, 8):
                term_copy(d, t - 1).start()

        for i in range(4):
            acc[pl.ds(i * TB, TB), :] = jnp.dot(
                tiles[i * 17 + 16], panel[par, 0, pl.ds(i * TB, TB), :],
                preferred_element_type=jnp.float32)
        acc[pl.ds(ROWS, 16), :] = jnp.zeros((16, TB), jnp.float32)

        @pl.when(t > 0)
        def _():
            finish_sends(1 - par)

        for place, h in (((3, 0), 0), ((1, 0), 1), ((0, 3), 0), ((0, 1), 1),
                         ((3, 0), 1), ((1, 0), 0), ((0, 3), 1), ((0, 1), 0)):
            pass_on(place, h)

        @pl.when(t == 0)
        def _():
            @pl.loop(1, 32)
            def _(d):
                column_copy(d).wait()

        add_up(0, 1)
        take_sibling(PLACES[:1])
        add_up(NEAR, NEAR + 1)
        add_up(1, 5)
        pass_on((2, 0), 0)
        pass_on((2, 0), 1)
        take_sibling(PLACES[1:5])
        add_up(NEAR + 1, NEAR + 5)
        pass_on((0, 2), 0)
        pass_on((0, 2), 1)
        for place, h in (((3, 3), 0), ((3, 1), 0), ((1, 1), 1), ((1, 3), 1),
                         ((3, 3), 1), ((3, 1), 1), ((1, 1), 0), ((1, 3), 0)):
            pass_on(place, h)
        add_up(5, 9)
        for place, h in (((2, 3), 0), ((2, 1), 1), ((2, 3), 1), ((2, 1), 0)):
            pass_on(place, h)
        add_up(9, 11)
        take_sibling(PLACES[5:11])
        add_up(NEAR + 5, NEAR + 9)
        for place in PLACES[13:15]:
            for h in (0, 1):
                pass_on(place, h)
        add_up(NEAR + 9, NEAR + 11)
        add_up(11, 15)
        for h in (0, 1):
            pass_on((2, 2), h)
        take_sibling(PLACES[11:15])
        add_up(NEAR + 11, NEAR + 15)
        add_up(15, 16)
        take_sibling(PLACES[15:])
        add_up(NEAR + 15, NEAR + 16)

        panel[1 - par, 0] = acc[pl.ds(0, ROWS), :].astype(jnp.bfloat16)
        low = acc[pl.ds(ROWS, 8), :] + acc[pl.ds(ROWS + 8, 8), :]
        terms[t] = low + pltpu.roll(low, 4, 0)

    for d in range(1, 8):
        term_copy(d, ITERS - 1).start()
    final_ref[...] = panel[ITERS % 2, 0]
    others[0] = terms[...]
    finish_sends((ITERS - 1) % 2)

    @pl.loop(0, ITERS)
    def _(t):
        for d in range(1, 8):
            term_copy(d, t).wait()
    turn = lax.rem(TB - z * 16, TB)
    for q in range(8):
        total = jnp.zeros((ITERS, 8, TB), jnp.float32)
        for d in range(8):
            total += weights_ref[q, lax.rem(z + 8 - d, 8)] * others[d]
        mixed_ref[q] = pltpu.roll(total, turn, 2)[:, :4, :16]


def shards(tile_data, tile_slots, requests, start_panel, projectors, combine_weights):
    r = lax.axis_index("row")
    c = r % 2
    y = (r // 2) % 4
    x = r // 8
    da = jnp.asarray(np.array([place[0] for place in PLACES] * 2, np.int32))
    db = jnp.asarray(np.array([place[1] for place in PLACES] * 2, np.int32))
    core = jnp.where(jnp.arange(32) < NEAR, c, 1 - c)
    x_at = (x + da * (1 - core) + db * core) % 4
    y_at = (y + da * core + db * (1 - core)) % 4
    source = (x_at * 4 + y_at) * 2 + core
    names = (source[:, None] * 2 + jnp.arange(2)[None, :]).reshape(64)
    flat_slots = tile_slots.reshape(68)
    spots = jnp.arange(68, dtype=jnp.int32)
    where_is = jnp.sum(jnp.where(flat_slots[None, :] == names[:, None], spots[None, :], 0), axis=1)
    own_wants = lax.dynamic_index_in_dim(requests, r, 1, keepdims=False).reshape(64)
    pick = jnp.sum(jnp.where(jnp.arange(64)[None, :] == names[:, None], own_wants[None, :], 0), axis=1)
    meta = jnp.concatenate([where_is, where_is // 17 * 4 + pick, (r - source + 32) % 32]).astype(jnp.int32)
    anywhere = pl.BlockSpec(memory_space=pl.ANY)
    small = pl.BlockSpec(memory_space=pltpu.SMEM)
    full = pl.BlockSpec(memory_space=pltpu.VMEM)
    dma = pltpu.SemaphoreType.DMA
    mixed, final = pl.pallas_call(
        kernel,
        out_shape=(
            jax.ShapeDtypeStruct((8, ITERS, 4, 16), jnp.float32),
            jax.ShapeDtypeStruct((ROWS, TB), jnp.bfloat16),
        ),
        in_specs=[small, small, anywhere, anywhere, anywhere],
        out_specs=(full, full),
        scratch_shapes=[
            pltpu.VMEM((2, 32, ROWS, TB), jnp.bfloat16),
            pltpu.VMEM((32, 16, ROWS), jnp.bfloat16),
            pltpu.VMEM((68, TB, TB), jnp.bfloat16),
            pltpu.VMEM((ROWS, TB), jnp.bfloat16),
            pltpu.VMEM((ROWS, TB), jnp.bfloat16),
            pltpu.VMEM((32, 16, TB), jnp.bfloat16),
            pltpu.VMEM((EXT, TB), jnp.float32),
            pltpu.VMEM((ITERS, 8, TB), jnp.float32),
            pltpu.VMEM((8, ITERS, 8, TB), jnp.float32),
            dma((3,)), dma((2, 2, 2)), dma((2, 2)), dma((2, 4, 2, 2)), dma((2, 4, 2)), dma((2, 16, 2)),
            dma((2, 16, 2)), dma((2, 16, 2)), dma((32,)), dma((32,)), dma((8, ITERS)), dma((8, ITERS)),
        ],
        compiler_params=pltpu.CompilerParams(collective_id=0, has_side_effects=True),
    )(meta, combine_weights, tile_data.reshape(68, TB, TB), start_panel.reshape(ROWS, TB),
      projectors.reshape(ROWS, TB))
    return mixed, final.reshape(1, ROWS, TB)


def solution(mesh):
    return jax.shard_map(
        shards,
        mesh=mesh,
        in_specs=(
            P("prime", "row", None, None, None),
            P("prime", "row", None),
            P("prime", None, None, None),
            P("prime", "row", None),
            P("prime", "row", None),
            P(),
        ),
        out_specs=(P(None, None, "row", "prime"), P("prime", "row", None)),
        check_vma=False,
    )
```
